32 devices in a mesh: groups: 2 (over x), expert: 16 (over z, y, core).
Axes of the slice: x: 2, y: 2, z: 4, core: 2. Of those that a mesh axis runs over, the one named last changes fastest.
Arguments:
- tokens: bfloat16 [256, 7168], P(('groups', 'expert')), parts along dimension 0, may hold values from -6 to 6
- expert_ids: int32 [256, 2], P(('groups', 'expert')), parts along dimension 0, may hold values from 0 to 3, as said below
- gate_scores: float32 [256, 2], P(('groups', 'expert')), parts along dimension 0, may hold values from 0.2 to 1
- w_gate_up: bfloat16 [16, 7168, 512], P('expert'), may hold values from -0.0625 to 0.0625
- w_down: bfloat16 [16, 256, 7168], P('expert'), may hold values from -0.1875 to 0.1875
Outputs:
- moe_out: bfloat16 [256, 7168], P(('groups', 'expert')), parts along dimension 0
The draws below stay inside these ranges and needn't reach their ends.
There are 2 independent parts, one for each index of `groups`. The reference program is written for one: setup_inputs(seed, part) draws one part's arguments, and reference() takes and returns one part's arrays. A program takes and returns all parts, laid end to end along the dimension named above; an argument that names none is the same for every part. Nothing has to cross between parts.
Inputs may be any that keep to these rules, and one draw needn't show every extreme that they name: `expert_ids`: each row names 2 different experts. In each aligned block of 8 rows (the rows of one device) no expert is named by more than 8 rows, and one expert is named by exactly 8 rows in every block.
All inputs are finite; a program needn't handle non-finite values.
Results may differ from the reference program's by a relative error of at most 0.0058.
Values may be sent and summed in bfloat16 or wider, within the bound.
A program may use at most 128 MiB of HBM per device.

```python
import math
import jax
import jax.numpy as jnp
from jax import lax

D = 7168
FH = 1024
SPLIT = 4
FH_DEV = 256
ROWS_DEV = 8
EXPERTS = 4
TOP = 2
ROWS = 128
CAP = 8
N_EXPERT = 16


def draw_expert_ids(key, part):
    key_hot, key_perm, key_split = jax.random.split(jax.random.fold_in(key, 11), 3)
    hottest = jax.random.randint(key_hot, (), 0, EXPERTS)
    perm_keys = jax.random.split(key_perm, N_EXPERT)
    others = jax.vmap(lambda subkey: jax.random.permutation(subkey, EXPERTS - 1))(perm_keys)
    ranking = jnp.concatenate([jnp.zeros((N_EXPERT, 1), jnp.int32), (others + 1).astype(jnp.int32)], axis=1)
    ranking = (ranking + hottest) % EXPERTS
    pair_count = EXPERTS // 2
    minor_share = jax.random.randint(key_split, (N_EXPERT, pair_count), 0, CAP // 2 + 1)
    minor_share = jnp.where(jnp.arange(pair_count)[None, :] == 0, 0, minor_share)
    row_index = jnp.arange(ROWS_DEV)[:, None]
    route_index = jnp.arange(TOP)[None, :]
    position = row_index + route_index * ROWS_DEV
    pair_index = position // CAP
    offset = position % CAP
    block_index = jnp.arange(N_EXPERT)[:, None, None]
    major_limit = CAP - minor_share[block_index, pair_index[None, :, :]]
    chosen = 2 * pair_index[None, :, :] + (offset[None, :, :] >= major_limit).astype(jnp.int32)
    drawn_ids = ranking[block_index, chosen]
    return drawn_ids.reshape(N_EXPERT * ROWS_DEV, TOP).astype(jnp.int32)


def steps_of(own_key, shape, cuts, least, top_value):
    loudness = 1.0
    for dim, blocks in cuts:
        steps = jax.random.uniform(jax.random.fold_in(jax.random.fold_in(own_key, 6), dim), (blocks,), jnp.float32, least / len(cuts), top_value / len(cuts))
        loudness = loudness * jnp.repeat(jnp.exp(steps), shape[dim] // blocks).reshape((-1,) + (1,) * (len(shape) - 1 - dim))
    return loudness


def noise(own_key, shape, width, reach, pieces=(), kind=jnp.bfloat16):
    result = width * jax.random.normal(own_key, shape, jnp.float32)
    if pieces:
        result = result * steps_of(own_key, shape, pieces, -0.22, 0.18)
    return jnp.clip(result, -reach, reach).astype(kind)


def setup_inputs(seed: int = 0, part: int = 0) -> dict:
    splits = jax.random.split(jax.random.key(seed), 6)
    part_splits = jax.random.split(jax.random.fold_in(splits[5], part), 6)
    tokens = noise(part_splits[0], (ROWS, D), 1.0, 6.0, ((0, 16),))
    expert_ids = draw_expert_ids(jax.random.fold_in(jax.random.fold_in(splits[5], part), 71), part)
    gate_scores = jnp.clip(jnp.exp(math.log(1.0) - 1.609438 * jax.random.uniform(part_splits[2], (ROWS, TOP), jnp.float32) ** steps_of(part_splits[2], (ROWS, TOP), ((0, 16),), -0.2, 0.2)), 0.2, 1.0)
    w_gate_up = noise(splits[3], (N_EXPERT, D, 2 * FH_DEV), D ** -0.5, 0.0625, ((0, 16),))
    w_down = noise(splits[4], (N_EXPERT, FH_DEV, D), FH ** -0.5, 0.1875, ((0, 16),))
    return dict(tokens=tokens, expert_ids=expert_ids, gate_scores=gate_scores, w_gate_up=w_gate_up, w_down=w_down)


def expert_block(block_tokens, gate_up_part, down_part):
    hidden_width = down_part.shape[0]
    gate_up = jnp.dot(block_tokens, gate_up_part, preferred_element_type=jnp.float32)
    hidden = (jax.nn.silu(gate_up[:, :hidden_width]) * gate_up[:, hidden_width:]).astype(jnp.bfloat16)
    return jnp.dot(hidden, down_part, preferred_element_type=jnp.float32).astype(jnp.bfloat16)


def reference(tokens, expert_ids, gate_scores, w_gate_up, w_down):
    row_count = expert_ids.shape[0]
    route_count = expert_ids.shape[1]
    route_weight = 2.5 * gate_scores / jnp.sum(gate_scores, axis=1, keepdims=True)
    flat_ids = expert_ids.reshape(-1)
    flat_weights = route_weight.reshape(-1)
    capacity_rows = N_EXPERT * CAP
    empty_index = row_count * route_count

    def add_expert(running, expert_index):
        chosen = jnp.nonzero(flat_ids == expert_index, size=capacity_rows, fill_value=empty_index)[0].astype(jnp.int32)
        row_index = chosen // route_count
        block_tokens = jnp.take(tokens, row_index, axis=0, mode="fill", fill_value=0)
        summed = jnp.zeros((capacity_rows, tokens.shape[1]), jnp.float32)
        for share in range(SPLIT):
            slot = expert_index * SPLIT + share
            summed = summed + expert_block(block_tokens, w_gate_up[slot], w_down[slot]).astype(jnp.float32)
        weight_of = jnp.take(flat_weights, chosen, mode="fill", fill_value=0.0)
        contribution = weight_of[:, None] * summed
        running = running.at[row_index].add(contribution, mode="drop")
        return running, None

    start = jnp.zeros((row_count, tokens.shape[1]), jnp.float32)
    running, _ = lax.scan(add_expert, start, jnp.arange(EXPERTS, dtype=jnp.int32))
    return running.astype(jnp.bfloat16)
```

```python
import functools
import jax
import jax.numpy as jnp
from jax import lax
from jax.experimental import pallas as pl
from jax.experimental.pallas import tpu as pltpu
from jax.sharding import PartitionSpec as P

SPLIT = 4
ROUTE_SCALE = 2.5
W1_PIECES = 4
W2_PIECES = 2
BF16 = jnp.bfloat16
F32 = jnp.float32


def kernel(planes, down_cols, tok_ref, ids_ref, score_ref, w1_hbm, w2_hbm, out_ref,
           x, s, w1, w2, part, r1, ysend, r2, zsend, r3, own,
           snd, rcv, wsem, tsem):
    rows, width = tok_ref.shape
    hidden_width = w2.shape[0]
    me = lax.axis_index("expert")
    p = me // SPLIT
    q = me % SPLIT
    y = q // 2
    c = q % 2
    ypeer = p * SPLIT + (1 - y) * 2 + c
    cpeer = p * SPLIT + y * 2 + (1 - c)
    qy = (1 - y) * 2 + c

    tok_copy = pltpu.make_async_copy(tok_ref, x.at[p, q], tsem)
    tok_copy.start()
    depth1 = w1.shape[0] // W1_PIECES
    depth2 = w2.shape[0] // W2_PIECES
    w1_copies = [
        pltpu.make_async_copy(w1_hbm.at[0, pl.ds(i * depth1, depth1)],
                              w1.at[pl.ds(i * depth1, depth1)], wsem.at[i])
        for i in range(W1_PIECES)
    ]
    w2_copies = [
        pltpu.make_async_copy(w2_hbm.at[0, pl.ds(i * depth2, depth2)],
                              w2.at[pl.ds(i * depth2, depth2)], wsem.at[W1_PIECES + i])
        for i in range(W2_PIECES)
    ]

    barrier = pltpu.get_barrier_semaphore()

    def greet(idx):
        pl.semaphore_signal(barrier, inc=1, device_id={"expert": idx},
                            device_id_type=pl.DeviceIdType.MESH)

    greet(cpeer)
    greet(ypeer)

    @pl.when(p > 0)
    def _():
        greet(me - SPLIT)

    @pl.when(p < planes - 1)
    def _():
        greet(me + SPLIT)

    for cp in w1_copies + w2_copies:
        cp.start()

    scores = score_ref[...]
    weights = ROUTE_SCALE * scores / jnp.sum(scores, axis=1, keepdims=True)
    lanes = s.shape[-1]
    lane = lax.broadcasted_iota(jnp.int32, (rows, lanes), 1)
    row = lax.broadcasted_iota(jnp.int32, (rows, lanes), 0)
    table = jnp.zeros((rows, lanes), F32)
    for k in range(ids_ref.shape[1]):
        table = table + jnp.where(lane == ids_ref[:, k:k + 1] * rows + row,
                                  weights[:, k:k + 1], 0.0)
    s[p, q] = jnp.sum(table, axis=0, keepdims=True)

    tok_copy.wait()
    neighbours = (2 + jnp.where(p > 0, 1, 0) + jnp.where(p < planes - 1, 1, 0)).astype(jnp.int32)
    pl.semaphore_wait(barrier, neighbours)

    def remote(src, dst, kind, rkind, plane, rplane, target):
        return pltpu.make_async_remote_copy(
            src_ref=src, dst_ref=dst, send_sem=snd.at[kind, plane],
            recv_sem=rcv.at[rkind, rplane], device_id={"expert": target},
            device_id_type=pl.DeviceIdType.MESH)

    def gather_copy(kind, plane):
        col = qy if kind == 4 else q
        target = (me + SPLIT, me - SPLIT, ypeer, cpeer, cpeer)[kind]
        rkind = 0 if kind == 1 else kind
        return (
            remote(x.at[plane, col], x.at[plane, col], kind, rkind, plane, plane, target),
            remote(s.at[plane, col], s.at[plane, col], kind + 5, rkind + 5, plane, plane, target),
        )

    def start(kind, plane):
        for cp in gather_copy(kind, plane):
            cp.start()

    def wait_recv(kind, plane):
        for cp in gather_copy(kind, plane):
            cp.wait_recv()

    def wait_send(kind, plane):
        for cp in gather_copy(kind, plane):
            cp.wait_send()

    low = jnp.minimum(p, planes - 1 - p)

    def plane_of(t):
        near = (t + 1) // 2
        alt = jnp.where(t % 2 == 1, p - near, p + near)
        far = t - low
        tail = jnp.where(p < planes - 1 - p, p + far, p - far)
        return jnp.where(t <= 2 * low, alt, tail)

    def goes_up(plane):
        return jnp.logical_and(plane <= p, p < planes - 1)

    def goes_down(plane):
        return jnp.logical_and(plane >= p, p > 0)

    def stage_a(t):
        plane = plane_of(t)

        @pl.when(plane != p)
        def _():
            wait_recv(0, plane)

        @pl.when(goes_up(plane))
        def _():
            start(0, plane)

        @pl.when(goes_down(plane))
        def _():
            start(1, plane)

        start(2, plane)
        start(3, plane)

    def stage_b(t):
        plane = plane_of(t)
        wait_recv(2, plane)
        start(4, plane)

    def core_copy(plane):
        return remote(part.at[plane, 1 - c], r1.at[plane], 10, 10, plane, plane, cpeer)

    def y_copy(plane):
        return remote(ysend.at[plane], r2.at[plane], 11, 11, plane, plane, ypeer)

    def z_copy(plane):
        return remote(zsend.at[plane], r3.at[p], 12, 12, plane, p, plane * SPLIT + q)

    def stage_c(t):
        plane = plane_of(t)
        wait_recv(3, plane)
        wait_recv(4, plane)
        block = x[plane].reshape(SPLIT * rows, width)
        gate_up = jnp.dot(block, w1[...], preferred_element_type=F32)
        gate = gate_up[:, :hidden_width]
        hidden = (gate / (1.0 + jnp.exp(-gate)) * gate_up[:, hidden_width:]).astype(BF16)
        chunk_s = jnp.broadcast_to(s[plane], (SPLIT, rows, lanes))
        lane3 = lax.broadcasted_iota(jnp.int32, (SPLIT, rows, lanes), 2)
        row3 = lax.broadcasted_iota(jnp.int32, (SPLIT, rows, lanes), 1)
        scale = jnp.sum(jnp.where(lane3 == p * rows + row3, chunk_s, 0.0), axis=2, keepdims=True)
        scale = scale.reshape(SPLIT * rows, 1)
        for j in range(width // down_cols):
            cols = pl.ds(j * down_cols, down_cols)
            res = jnp.dot(hidden, w2[:, cols], preferred_element_type=F32) * scale
            res = res.astype(BF16)
            for b in range(SPLIT):
                part[plane, b % 2, b // 2, :, cols] = res[b * rows:(b + 1) * rows]
        core_copy(plane).start()

    def stage_d(t):
        plane = plane_of(t)
        core_copy(plane).wait_recv()
        ysend[plane] = (part[plane, c, 1 - y].astype(F32)
                        + r1[plane, 1 - y].astype(F32)).astype(BF16)
        y_copy(plane).start()

    def stage_e(t):
        plane = plane_of(t)
        y_copy(plane).wait_recv()
        total = (part[plane, c, y].astype(F32) + r1[plane, y].astype(F32)
                 + r2[plane].astype(F32))

        @pl.when(plane == p)
        def _():
            own[...] = total

        @pl.when(plane != p)
        def _():
            zsend[plane] = total.astype(BF16)
            z_copy(plane).start()

    stage_a(0)
    stage_a(1)
    stage_b(0)
    for cp in w1_copies + w2_copies:
        cp.wait()

    def step(i, carry):
        stage_c(i)

        @pl.when(i + 2 < planes)
        def _():
            stage_a(i + 2)

        @pl.when(i + 1 < planes)
        def _():
            stage_b(i + 1)

        @pl.when(i > 0)
        def _():
            stage_e(i - 1)

        stage_d(i)
        return carry

    lax.fori_loop(0, planes, step, 0)
    stage_e(planes - 1)

    def drain(plane, carry):
        @pl.when(goes_up(plane))
        def _():
            wait_send(0, plane)

        @pl.when(goes_down(plane))
        def _():
            wait_send(1, plane)

        for kind in (2, 3, 4):
            wait_send(kind, plane)
        core_copy(plane).wait_send()
        y_copy(plane).wait_send()
        return carry

    lax.fori_loop(0, planes, drain, 0)

    def collect(k, carry):
        plane = lax.rem(p + k, planes)
        remote(zsend.at[plane], r3.at[plane], 12, 12, plane, plane, plane * SPLIT + q).wait()
        own[...] += r3[plane].astype(F32)
        return carry

    lax.fori_loop(1, planes, collect, 0)
    out_ref[...] = own[...].astype(BF16)


def body(tokens, expert_ids, gate_scores, w_gate_up, w_down):
    dev_count = lax.axis_size("expert")
    planes = dev_count // SPLIT
    rows, width = tokens.shape
    hidden_width = w_down.shape[1]
    lanes = -(-planes * rows // 128) * 128
    down_cols = 1024 if width % 1024 == 0 else 128
    blk = (rows, width)
    vmem = pl.BlockSpec(memory_space=pltpu.VMEM)
    hbm = pl.BlockSpec(memory_space=pl.ANY)
    return pl.pallas_call(
        functools.partial(kernel, planes, down_cols),
        out_shape=jax.ShapeDtypeStruct(blk, BF16),
        in_specs=[hbm, vmem, vmem, hbm, hbm],
        out_specs=vmem,
        scratch_shapes=[
            pltpu.VMEM((planes, SPLIT) + blk, BF16),
            pltpu.VMEM((planes, SPLIT, 1, lanes), F32),
            pltpu.VMEM((width, 2 * hidden_width), BF16),
            pltpu.VMEM((hidden_width, width), BF16),
            pltpu.VMEM((planes, 2, 2) + blk, BF16),
            pltpu.VMEM((planes, 2) + blk, BF16),
            pltpu.VMEM((planes,) + blk, BF16),
            pltpu.VMEM((planes,) + blk, BF16),
            pltpu.VMEM((planes,) + blk, BF16),
            pltpu.VMEM((planes,) + blk, BF16),
            pltpu.VMEM(blk, F32),
            pltpu.SemaphoreType.DMA((13, planes)),
            pltpu.SemaphoreType.DMA((13, planes)),
            pltpu.SemaphoreType.DMA((W1_PIECES + W2_PIECES,)),
            pltpu.SemaphoreType.DMA,
        ],
        compiler_params=pltpu.CompilerParams(
            collective_id=0, has_side_effects=True, vmem_limit_bytes=63 * 1024 * 1024),
        name="expert_layer",
    )(tokens, expert_ids, gate_scores, w_gate_up, w_down)


def solution(mesh):
    rows = P(("groups", "expert"), None)
    weights = P("expert", None, None)
    return jax.shard_map(body, mesh=mesh, in_specs=(rows, rows, rows, weights, weights),
                         out_specs=rows, check_vma=False)
```
